256 devices in a mesh: site: 16 (over y, z_lo), cuts: 16 (over z_hi, x, core).
Axes of the slice: x: 4, y: 4, z: 8 (z_hi: 2, z_lo: 4; z = z_hi * 4 + z_lo), core: 2. Of those that a mesh axis runs over, the one named last changes fastest.
Arguments:
- eigen_vectors: bfloat16 [32, 2, 3, 256, 9216], P('cuts', None, None, None, 'site'), may hold values from -6 to 6
- perambulators: bfloat16 [512, 2, 1024, 512], P(('site', 'cuts')), may hold values from -0.049804688 to 0.049804688
- momenta: int32 [3, 3], replicated, may hold values from 1 to 3
- source_slice: int32 [1], replicated, may hold values from 0 to 31
- sink_slices: int32 [512], P(('site', 'cuts')), may hold values from 0 to 1
- sink_momenta: int32 [512], P(('site', 'cuts')), may hold values from 0 to 2
- spin_order: int32 [4], replicated, may hold values from 0 to 3, each once
Outputs:
- correlators: bfloat16 [512, 2, 512, 512], P(('site', 'cuts'))
The draws below stay inside these ranges and needn't reach their ends.
Inputs may be any that keep to these rules, and one draw needn't show every extreme that they name: `spin_order`: a permutation of 0 to 3.
All inputs are finite; a program needn't handle non-finite values.
Results may differ from the reference program's by a relative error of at most 0.0081.
Values may be sent and summed in bfloat16 or wider, within the bound.
No kernel may reach another device: no remote copies, remote signals or barrier semaphores. Data moves between devices by JAX's collectives and lax.ppermute only.
A program may use at most 64 MiB of HBM per device.

```python
import math
import jax
import jax.numpy as jnp
from jax import lax

NVEC = 256
L = 96
PLANES = 1
TSL_DEV = 2
NMOM = 3
SNK_DEV = 2
SITES = 9216
TSL = 32
SINKS = 512
N_CUTS = 16


def set_ends(values, key, low, top_value):
    place = [jax.random.randint(jax.random.fold_in(key, axis), (), 0, length) for axis, length in enumerate(values.shape)]
    longest = values.shape.index(max(values.shape))
    beside = place[:longest] + [(place[longest] + 1) % values.shape[longest]] + place[longest + 1:]
    return values.at[tuple(place)].set(low).at[tuple(beside)].set(top_value)


def steps_of(stream_key, extent, pieces, least, high):
    loudness, own = 1.0, jax.random.fold_in(stream_key, 6)
    for axis_at, shards_of in pieces:
        steps = jnp.exp(jax.random.uniform(jax.random.fold_in(own, axis_at), (shards_of,), jnp.float32, least / len(pieces), high / len(pieces)))
        loudness = loudness * jnp.repeat(steps, extent[axis_at] // shards_of).reshape([-1 if axis == axis_at else 1 for axis in range(len(extent))])
    return loudness


def centred(rng, shape, scale, reach, pieces=(), kind=jnp.bfloat16):
    level = steps_of(rng, shape, pieces, -0.22, 0.18) if pieces else 1.0
    result = jax.random.normal(rng, shape, jnp.float32) * scale * level
    return jnp.minimum(jnp.maximum(result, -reach), reach).astype(kind)


def setup_inputs(seed: int = 0) -> dict:
    streams_of = jax.random.split(jax.random.key(seed), 8)
    return {
        "eigen_vectors": centred(streams_of[0], (TSL, 2, 3, NVEC, SITES), 1.0, 6.0, ((0, 16), (4, 16))),
        "perambulators": centred(streams_of[1], (SINKS, 2, 4 * NVEC, 2 * NVEC), 0.0078125, 0.049804688, ((0, 256),)),
        "momenta": set_ends(jax.random.randint(streams_of[2], (NMOM, 3), 1, 4), jax.random.fold_in(streams_of[2], 1), 1, 3).astype(jnp.int32),
        "source_slice": jax.random.randint(streams_of[3], (1,), 0, TSL).astype(jnp.int32),
        "sink_slices": set_ends(jax.random.randint(streams_of[4], (SINKS,), 0, TSL_DEV), jax.random.fold_in(streams_of[4], 1), 0, TSL_DEV - 1).astype(jnp.int32),
        "sink_momenta": set_ends(jax.random.randint(streams_of[5], (SINKS,), 0, NMOM), jax.random.fold_in(streams_of[5], 1), 0, NMOM - 1).astype(jnp.int32),
        "spin_order": jax.random.permutation(streams_of[6], 4).astype(jnp.int32),
    }


def spin_table():
    return 0.5 * jnp.array([[1.0, 1.0, 1.0, 1.0], [1.0, -1.0, 1.0, -1.0], [1.0, 1.0, -1.0, -1.0], [1.0, -1.0, -1.0, 1.0]], jnp.float32)

def dilution_mix(spin_order):
    picked = (spin_order[:2, None] == jnp.arange(4, dtype=jnp.int32)[None, :]).astype(jnp.float32)
    inner = jnp.dot(picked, spin_table(), precision=lax.Precision.HIGHEST)
    return jnp.dot(inner, picked.T, precision=lax.Precision.HIGHEST)

def phase_tables(momenta, first_site, count):
    global_site = first_site + jnp.arange(count, dtype=jnp.int32)
    coord_x = global_site % L
    coord_y = global_site // L % L
    coord_z = global_site // (L * L)
    winding = (momenta[:, 0:1] * coord_x[None, :] + momenta[:, 1:2] * coord_y[None, :] + momenta[:, 2:3] * coord_z[None, :]) % L
    theta = 2.0 * math.pi / L * winding.astype(jnp.float32)
    return (jnp.cos(theta), jnp.sin(theta))

def rounded(value):
    return lax.optimization_barrier(value.astype(jnp.bfloat16)).astype(jnp.float32)

def slice_elementals(vectors, cosine, sine):
    real_part = vectors[0].astype(jnp.float32)
    imag_part = vectors[1].astype(jnp.float32)
    cos_wide = cosine[:, None, None, :]
    sin_wide = sine[:, None, None, :]
    phased_re = rounded(cos_wide * real_part[None] + sin_wide * imag_part[None])
    phased_im = rounded(cos_wide * imag_part[None] - sin_wide * real_part[None])
    elem_re = jnp.einsum('cix,pcjx->pij', real_part, phased_re) + jnp.einsum('cix,pcjx->pij', imag_part, phased_im)
    elem_im = jnp.einsum('cix,pcjx->pij', real_part, phased_im) - jnp.einsum('cix,pcjx->pij', imag_part, phased_re)
    scale = 1.0 / math.sqrt(6.0 * L * L * PLANES)
    return scale * jnp.stack([elem_re, elem_im], axis=1)

def contract(perambulator, source_el, sink_el, mixing):
    count = perambulator.shape[0]
    nvec = source_el.shape[-1]
    peram_re = perambulator[:, 0].astype(jnp.float32).reshape(count, 4, nvec, 2 * nvec)
    peram_im = perambulator[:, 1].astype(jnp.float32).reshape(count, 4, nvec, 2 * nvec)
    src_re = source_el[:, 0].astype(jnp.float32)
    src_im = source_el[:, 1].astype(jnp.float32)
    left_re = rounded(jnp.einsum('kij,ksjb->ksib', src_re, peram_re) - jnp.einsum('kij,ksjb->ksib', src_im, peram_im))
    left_im = rounded(jnp.einsum('kij,ksjb->ksib', src_re, peram_im) + jnp.einsum('kij,ksjb->ksib', src_im, peram_re))
    flipped_re = jnp.stack([left_re[:, 2], left_re[:, 3], -left_re[:, 0], -left_re[:, 1]], axis=1)
    flipped_im = jnp.stack([left_im[:, 2], left_im[:, 3], -left_im[:, 0], -left_im[:, 1]], axis=1)
    middle_re = rounded(jnp.einsum('ksab,ksac->kbc', peram_re, flipped_re) + jnp.einsum('ksab,ksac->kbc', peram_im, flipped_im))
    middle_im = rounded(jnp.einsum('ksab,ksac->kbc', peram_re, flipped_im) - jnp.einsum('ksab,ksac->kbc', peram_im, flipped_re))
    blocks_re = middle_re.reshape(count, 2 * nvec, 2, nvec)
    blocks_im = middle_im.reshape(count, 2 * nvec, 2, nvec)
    snk_re = sink_el[:, 0].astype(jnp.float32)
    snk_im = sink_el[:, 1].astype(jnp.float32)
    inner_re = jnp.einsum('kbej,kjc->kbec', blocks_re, snk_re) - jnp.einsum('kbej,kjc->kbec', blocks_im, snk_im)
    inner_im = jnp.einsum('kbej,kjc->kbec', blocks_re, snk_im) + jnp.einsum('kbej,kjc->kbec', blocks_im, snk_re)
    out_re = jnp.einsum('kbec,ef->kbfc', inner_re, mixing, precision=lax.Precision.HIGHEST).reshape(count, 2 * nvec, 2 * nvec)
    out_im = jnp.einsum('kbec,ef->kbfc', inner_im, mixing, precision=lax.Precision.HIGHEST).reshape(count, 2 * nvec, 2 * nvec)
    return jnp.stack([out_re, out_im], axis=1).astype(jnp.bfloat16)

def reference(eigen_vectors, perambulators, momenta, source_slice, sink_slices, sink_momenta, spin_order):
    cosine, sine = phase_tables(momenta, jnp.int32(0), SITES)
    elementals = lax.map(lambda vectors: slice_elementals(vectors, cosine, sine), eigen_vectors)
    source_el = lax.dynamic_index_in_dim(elementals, source_slice[0], 0, keepdims=False).astype(jnp.bfloat16)
    mixing = dilution_mix(spin_order)
    sink_index = jnp.arange(SINKS, dtype=jnp.int32)
    owner_cut = sink_index // SNK_DEV % N_CUTS
    global_slice = (owner_cut * TSL_DEV + sink_slices).astype(jnp.int32)

    def one_sink(packed):
        peram, slice_id, moment_id = packed
        src = lax.dynamic_index_in_dim(source_el, moment_id, 0, keepdims=True)
        whole = lax.dynamic_index_in_dim(elementals, slice_id, 0, keepdims=False)
        snk = lax.dynamic_index_in_dim(whole, moment_id, 0, keepdims=True).astype(jnp.bfloat16)
        return contract(peram[None], src, snk, mixing)[0]
    return lax.map(one_sink, (perambulators, global_slice, sink_momenta))
```

```python
import math

import jax
import jax.numpy as jnp
from jax import lax
from jax.experimental import pallas as pl
from jax.experimental.pallas import tpu as pltpu
from jax.sharding import PartitionSpec as P

L = 96
PLANES = 1
NMOM = 3
NVEC = 256
YN = 4
ZN = 4
SCALE = 1.0 / math.sqrt(6.0 * L * L * PLANES)
F32 = jnp.float32
BF16 = jnp.bfloat16
NT = (((1,), (1,)), ((), ()))


def y_shift(step):
    return [(y * ZN + z, (y + step) % YN * ZN + z) for y in range(YN) for z in range(ZN)]


def z_shift(step):
    return [(y * ZN + z, y * ZN + (z + step) % ZN) for y in range(YN) for z in range(ZN)]


def cut_move(dh, dx, dc):
    return [
        (h * 8 + x * 2 + c, (h + dh) % 2 * 8 + (x + dx) % 4 * 2 + (c + dc) % 2)
        for h in range(2)
        for x in range(4)
        for c in range(2)
    ]


def sin_cos(winding):
    quarter = jnp.floor((winding + 12.5) * (1.0 / 24.0))
    angle = (winding - 24.0 * quarter) * (2.0 * math.pi / L)
    sq = angle * angle
    sine = angle * (1.0 + sq * (-1 / 6 + sq * (1 / 120 + sq * (-1 / 5040 + sq * (1 / 362880)))))
    cosine = 1.0 + sq * (
        -1 / 2 + sq * (1 / 24 + sq * (-1 / 720 + sq * (1 / 40320 + sq * (-1 / 3628800))))
    )
    odd = (quarter == 1.0) | (quarter == 3.0)
    cos_out = jnp.where(odd, sine, cosine)
    sin_out = jnp.where(odd, cosine, sine)
    cos_out = jnp.where((quarter == 1.0) | (quarter == 2.0), -cos_out, cos_out)
    sin_out = jnp.where((quarter == 2.0) | (quarter == 3.0), -sin_out, sin_out)
    return cos_out, sin_out


def elementals_kernel(sc, mom, v_ref, keep, send1, send2, send3, acc, trig):
    colour = pl.program_id(0)
    count = v_ref.shape[-1]

    @pl.when(colour == 0)
    def _():
        site = (sc[1] + lax.broadcasted_iota(jnp.int32, (1, count), 1)).astype(F32)
        row = jnp.floor((site + 0.5) * (1.0 / L))
        x = site - L * row
        z = jnp.floor((row + 0.5) * (1.0 / L))
        y = row - L * z
        for p in range(NMOM):
            turn = (
                mom[p, 0].astype(F32) * x + mom[p, 1].astype(F32) * y + mom[p, 2].astype(F32) * z
            )
            turn = turn - L * jnp.floor((turn + 0.5) * (1.0 / L))
            cosine, sine = sin_cos(turn)
            trig[p : p + 1, :] = cosine
            trig[p + 4 : p + 5, :] = sine

    both = v_ref[0, :, 0].reshape(2 * NVEC, count)
    real = v_ref[0, 0, 0].astype(F32)
    imag = v_ref[0, 1, 0].astype(F32)
    for p in range(NMOM):
        cosine = trig[p : p + 1, :]
        sine = trig[p + 4 : p + 5, :]
        phased_re = (cosine * real + sine * imag).astype(BF16)
        phased_im = (cosine * imag - sine * real).astype(BF16)
        with_re = lax.dot_general(both, phased_re, NT, preferred_element_type=F32)
        with_im = lax.dot_general(both, phased_im, NT, preferred_element_type=F32)
        out_re = with_re[:NVEC] + with_im[NVEC:]
        out_im = with_im[:NVEC] - with_re[NVEC:]

        @pl.when(colour == 0)
        def _():
            acc[p, 0] = out_re
            acc[p, 1] = out_im

        @pl.when(colour > 0)
        def _():
            acc[p, 0] += out_re
            acc[p, 1] += out_im

    @pl.when(colour == 2)
    def _():
        rows = NVEC // YN
        for step, out in enumerate((keep, send1, send2, send3)):
            first = pl.multiple_of((sc[2] + step) % YN * rows, rows)
            out[...] = (acc[:, :, pl.ds(first, rows), :] * SCALE).astype(out.dtype)


def partial_elementals(scalars, momenta, eigen_vectors):
    count = eigen_vectors.shape[-1]
    rows = NVEC // YN
    whole = lambda: pl.BlockSpec((NMOM, 2, rows, NVEC), lambda c, sc, mom: (0, 0, 0, 0))
    piece = lambda dtype: jax.ShapeDtypeStruct((NMOM, 2, rows, NVEC), dtype)
    return pl.pallas_call(
        elementals_kernel,
        grid_spec=pltpu.PrefetchScalarGridSpec(
            num_scalar_prefetch=2,
            grid=(3,),
            in_specs=[
                pl.BlockSpec((1, 2, 1, NVEC, count), lambda c, sc, mom: (sc[0], 0, c, 0, 0))
            ],
            out_specs=[whole(), whole(), whole(), whole()],
            scratch_shapes=[
                pltpu.VMEM((NMOM, 2, NVEC, NVEC), F32),
                pltpu.VMEM((8, count), F32),
            ],
        ),
        out_shape=[piece(F32), piece(BF16), piece(BF16), piece(BF16)],
        name="elementals",
    )(scalars, momenta, eigen_vectors)


def sum_kernel(sc, kept, got1, got2, got3, keep, send1, send2, send3):
    rows = NVEC // YN // ZN
    for step, out in enumerate((keep, send1, send2, send3)):
        first = pl.multiple_of((sc[3] + step) % ZN * rows, rows)
        part = kept[:, :, pl.ds(first, rows), :]
        for got in (got1, got2, got3):
            part = part + got[:, :, pl.ds(first, rows), :].astype(F32)
        out[...] = part.astype(out.dtype)


def sum_and_split(scalars, kept, got):
    rows = NVEC // YN // ZN
    piece = lambda dtype: jax.ShapeDtypeStruct((NMOM, 2, rows, NVEC), dtype)
    vmem = lambda: pl.BlockSpec(memory_space=pltpu.VMEM)
    return pl.pallas_call(
        sum_kernel,
        in_specs=[pl.BlockSpec(memory_space=pltpu.SMEM)] + [vmem() for _ in range(4)],
        out_specs=[vmem() for _ in range(4)],
        out_shape=[piece(F32), piece(BF16), piece(BF16), piece(BF16)],
        name="sum_split",
    )(scalars, kept, *got)


def flip_kernel(t_ref, out):
    for part in range(2):
        out[0, :, part * NVEC : (part + 1) * NVEC] = t_ref[0, part, 0].T


def transposed(perams):
    count, _, spins, nvec, columns = perams.shape
    return pl.pallas_call(
        flip_kernel,
        grid=(count, spins),
        in_specs=[pl.BlockSpec((1, 2, 1, nvec, columns), lambda k, s: (k, 0, s, 0, 0))],
        out_specs=pl.BlockSpec((1, columns, 2 * nvec), lambda k, s: (k, 0, s)),
        out_shape=jax.ShapeDtypeStruct((count, columns, spins * 2 * nvec), BF16),
        name="transpose_tau",
    )(perams)


def pick_kernel(idx, stack_a, stack_b, own, send1, send2, send3):
    for step, out in enumerate((own, send1, send2, send3)):
        for k in range(2):
            chosen = idx[step, k]
            is_a = chosen < NMOM
            at = jnp.where(is_a, chosen, chosen - NMOM)

            @pl.when(is_a)
            def _():
                out[k] = stack_a[:, at]

            @pl.when(jnp.logical_not(is_a))
            def _():
                out[k] = stack_b[:, at]


def pick_sinks(idx, stack_a, stack_b):
    rows = NVEC // YN // ZN
    vmem = lambda: pl.BlockSpec(memory_space=pltpu.VMEM)
    piece = jax.ShapeDtypeStruct((2, ZN, 2, rows, NVEC), BF16)
    return pl.pallas_call(
        pick_kernel,
        in_specs=[pl.BlockSpec(memory_space=pltpu.SMEM), vmem(), vmem()],
        out_specs=[vmem() for _ in range(4)],
        out_shape=[piece] * 4,
        name="pick_sinks",
    )(idx, stack_a, stack_b)


def contract_kernel(sc, mom, mix, f0, f1, f2, f3, s0, s1, s2, s3, t_ref, tt_ref, out, fmat, smat, gmat):
    k = pl.program_id(0)
    rows = NVEC // YN // ZN
    at = mom[k]
    for dy, (f_ref, s_ref) in enumerate(((f0, s0), (f1, s1), (f2, s2), (f3, s3))):
        for dz in range(ZN):
            first = (sc[2] + (YN - dy)) % YN * (ZN * rows) + (sc[3] + (ZN - dz)) % ZN * rows
            first = pl.multiple_of(first, rows)
            f_re = f_ref[dz, at, 0]
            f_im = f_ref[dz, at, 1]
            fmat[pl.ds(first, rows), :NVEC] = f_re
            fmat[pl.ds(first, rows), NVEC:] = -f_im
            fmat[pl.ds(NVEC + first, rows), :NVEC] = f_im
            fmat[pl.ds(NVEC + first, rows), NVEC:] = f_re
            s_re = s_ref[k, dz, 0]
            s_im = s_ref[k, dz, 1]
            smat[pl.ds(first, rows), :NVEC] = s_re
            smat[pl.ds(first, rows), NVEC:] = s_im
            smat[pl.ds(NVEC + first, rows), :NVEC] = -s_im
            smat[pl.ds(NVEC + first, rows), NVEC:] = s_re
    wide = t_ref.shape[-1]
    f_all = fmat[...]
    for spin in range(4):
        tau = t_ref[0, :, spin].reshape(2 * NVEC, wide)
        left = jnp.dot(f_all, tau, preferred_element_type=F32).astype(BF16)
        home = (spin + 2) % 4
        if home >= 2:
            left = -left
        base = home * 2 * NVEC
        gmat[base : base + NVEC, :wide] = left[:NVEC]
        gmat[base + NVEC : base + 2 * NVEC, :wide] = left[NVEC:]
        gmat[base : base + NVEC, wide:] = left[NVEC:]
        gmat[base + NVEC : base + 2 * NVEC, wide:] = -left[:NVEC]
    s_all = smat[...]
    middle = jnp.dot(tt_ref[0], gmat[...], preferred_element_type=F32).astype(BF16)
    inner = []
    for e in range(2):
        block = jnp.concatenate(
            [middle[:, e * NVEC : (e + 1) * NVEC], middle[:, wide + e * NVEC : wide + (e + 1) * NVEC]],
            axis=1,
        )
        inner.append(jnp.dot(block, s_all, preferred_element_type=F32))
    for f in range(2):
        mixed = inner[0] * mix[0, f] + inner[1] * mix[1, f]
        out[0, 0, :, f * NVEC : (f + 1) * NVEC] = mixed[:, :NVEC].astype(BF16)
        out[0, 1, :, f * NVEC : (f + 1) * NVEC] = mixed[:, NVEC:].astype(BF16)


def contract(scalars, momenta, mixing, source, sinks, perams, perams_t):
    count, _, spins, nvec, wide = perams.shape
    rows = NVEC // YN // ZN
    f_spec = lambda: pl.BlockSpec((ZN, NMOM, 2, rows, NVEC), lambda k, *_: (0, 0, 0, 0, 0))
    s_spec = lambda: pl.BlockSpec((count, ZN, 2, rows, NVEC), lambda k, *_: (0, 0, 0, 0, 0))
    return pl.pallas_call(
        contract_kernel,
        grid_spec=pltpu.PrefetchScalarGridSpec(
            num_scalar_prefetch=3,
            grid=(count,),
            in_specs=[f_spec() for _ in range(4)]
            + [s_spec() for _ in range(4)]
            + [
                pl.BlockSpec((1, 2, spins, nvec, wide), lambda k, *_: (k, 0, 0, 0, 0)),
                pl.BlockSpec((1, wide, spins * 2 * nvec), lambda k, *_: (k, 0, 0)),
            ],
            out_specs=pl.BlockSpec((1, 2, wide, wide), lambda k, *_: (k, 0, 0, 0)),
            scratch_shapes=[
                pltpu.VMEM((2 * NVEC, 2 * NVEC), BF16),
                pltpu.VMEM((2 * NVEC, 2 * NVEC), BF16),
                pltpu.VMEM((spins * 2 * nvec, 2 * wide), BF16),
            ],
        ),
        out_shape=jax.ShapeDtypeStruct((count, 2, wide, wide), BF16),
        name="contract",
    )(scalars, momenta, mixing, *source, *sinks, perams, perams_t)


def spin_table():
    return 0.5 * jnp.array(
        [
            [1.0, 1.0, 1.0, 1.0],
            [1.0, -1.0, 1.0, -1.0],
            [1.0, 1.0, -1.0, -1.0],
            [1.0, -1.0, -1.0, 1.0],
        ],
        F32,
    )


def dilution_mix(spin_order):
    picked = spin_order[:2, None] == jnp.arange(4, dtype=jnp.int32)[None, :]
    rows = jnp.sum(jnp.where(picked[:, :, None], spin_table()[None], 0.0), axis=1)
    return jnp.sum(jnp.where(picked[None], rows[:, None, :], 0.0), axis=2)


def body(
    eigen_vectors, perambulators, momenta, source_slice, sink_slices, sink_momenta, spin_order
):
    slab_slices = eigen_vectors.shape[0]
    site_count = eigen_vectors.shape[-1]
    site = lax.axis_index("site")
    cut = lax.axis_index("cuts")
    my_y = site // ZN
    my_z = site % ZN
    source = source_slice[0]
    root = source // slab_slices
    near = source % slab_slices
    lanes = jnp.arange(4, dtype=jnp.int32)

    def scalar_row(slice_id):
        return jnp.where(
            lanes == 0,
            slice_id,
            jnp.where(lanes == 1, site * site_count, jnp.where(lanes == 2, my_y, my_z)),
        )

    scal_a = scalar_row(near)
    scal_b = scalar_row(1 - near)

    far = (sink_slices != near).astype(jnp.int32)
    flat = far * NMOM + sink_momenta
    idx_far = [lax.ppermute(flat, "site", y_shift(-step)) for step in range(1, YN)]
    idx = jnp.stack([flat] + idx_far)

    def reduce_slice(scalars):
        kept, *sends = partial_elementals(scalars, momenta, eigen_vectors)
        got = [lax.ppermute(v, "site", y_shift(k + 1)) for k, v in enumerate(sends)]
        kept, *sends = sum_and_split(scalars, kept, got)
        got = [lax.ppermute(v, "site", z_shift(k + 1)) for k, v in enumerate(sends)]
        return (kept + sum(g.astype(F32) for g in got)).astype(BF16)

    def gather_z(own):
        return jnp.stack([own] + [lax.ppermute(own, "site", z_shift(k)) for k in range(1, ZN)])

    chunk_a = reduce_slice(scal_a)
    chunk_b = reduce_slice(scal_b)

    held = chunk_a
    my_x = cut // 2 % 4
    got = [lax.ppermute(held, "cuts", cut_move(0, k, 0)) for k in range(1, 4)]
    hop = (my_x - root // 2 % 4) % 4
    held = jnp.where(
        hop == 0, held, jnp.where(hop == 1, got[0], jnp.where(hop == 2, got[1], got[2]))
    )
    got = lax.ppermute(held, "cuts", cut_move(1, 0, 0))
    held = jnp.where(cut // 8 == root // 8, held, got)
    got = lax.ppermute(held, "cuts", cut_move(0, 0, 1))
    held = jnp.where(cut % 2 == root % 2, held, got)
    stack_f = gather_z(held)
    source_parts = [stack_f] + [lax.ppermute(stack_f, "site", y_shift(k)) for k in range(1, YN)]

    stack_a = gather_z(chunk_a)
    stack_b = gather_z(chunk_b)
    own, *sends = pick_sinks(idx, stack_a, stack_b)
    sink_parts = [own] + [lax.ppermute(v, "site", y_shift(k + 1)) for k, v in enumerate(sends)]

    count = perambulators.shape[0]
    perams = perambulators.reshape(count, 2, 4, NVEC, 2 * NVEC)
    perams_t = transposed(perams)
    mixing = dilution_mix(spin_order)
    return contract(scal_a, sink_momenta, mixing, source_parts, sink_parts, perams, perams_t)


def solution(mesh):
    placed = (
        P("cuts", None, None, None, "site"),
        P(("site", "cuts"), None, None, None),
        P(),
        P(),
        P(("site", "cuts")),
        P(("site", "cuts")),
        P(),
    )
    return jax.shard_map(
        body,
        mesh=mesh,
        in_specs=placed,
        out_specs=P(("site", "cuts"), None, None, None),
        check_vma=False,
    )
```

```python
import functools
import math

import jax
import jax.numpy as jnp
from jax import lax
from jax.experimental import pallas as pl
from jax.experimental.pallas import tpu as pltpu
from jax.sharding import PartitionSpec as P


L = 96
PLANES = 1
NMOM = 3
NVEC = 256
YN = 4
ZN = 4
SCALE = 1.0 / math.sqrt(6.0 * L * L * PLANES)
F32 = jnp.float32
BF16 = jnp.bfloat16


def y_swap(step):
    return [(y * ZN + z, (y ^ step) * ZN + z) for y in range(YN) for z in range(ZN)]


def z_swap(step):
    return [(y * ZN + z, y * ZN + (z ^ step)) for y in range(YN) for z in range(ZN)]


def cut_swap(dx, dc):
    return [
        (h * 8 + x * 2 + c, h * 8 + (x ^ dx) * 2 + (c ^ dc))
        for h in range(2)
        for x in range(4)
        for c in range(2)
    ]


def half_swap():
    return [
        ((y * ZN + z) * 16 + h * 8 + rest, (y * ZN + (z ^ 2)) * 16 + (h ^ 1) * 8 + rest)
        for y in range(YN)
        for z in range(ZN)
        for h in range(2)
        for rest in range(8)
    ]


def sin_cos(winding):
    quarter = jnp.floor((winding + 12.5) * (1.0 / 24.0))
    angle = (winding - 24.0 * quarter) * (2.0 * math.pi / L)
    sq = angle * angle
    sine = angle * (1.0 + sq * (-1 / 6 + sq * (1 / 120 + sq * (-1 / 5040 + sq * (1 / 362880)))))
    cosine = 1.0 + sq * (
        -1 / 2 + sq * (1 / 24 + sq * (-1 / 720 + sq * (1 / 40320 + sq * (-1 / 3628800))))
    )
    odd = (quarter == 1.0) | (quarter == 3.0)
    cos_out = jnp.where(odd, sine, cosine)
    sin_out = jnp.where(odd, cosine, sine)
    cos_out = jnp.where((quarter == 1.0) | (quarter == 2.0), -cos_out, cos_out)
    sin_out = jnp.where((quarter == 2.0) | (quarter == 3.0), -sin_out, sin_out)
    return cos_out, sin_out


def scalar_row(source, turned):
    near = source[0] % 2
    return near, (1 - near if turned else near)


def elementals_kernel(
    turned, source, mom, slices, moments, v_hbm, keep, send1, send2, send3, acc, trig, wide_trig, flipped, phased, vbuf, kbuf, sbuf, sems
):
    depth = vbuf.shape[1]
    count = depth // 3
    padded = flipped.shape[1]
    span = trig.shape[1]
    near, mine = scalar_row(source, turned)
    place = lax.axis_index("site")
    my_y = place // ZN
    loads = []
    for colour in range(3):
        rows = pl.ds(colour * count, count)
        load = pltpu.make_async_copy(
            v_hbm.at[mine, :, rows, :], vbuf.at[:, rows, :], sems.at[colour]
        )
        load.start()
        loads.append(load)
    site = (place * count + lax.broadcasted_iota(jnp.int32, (1, span), 1)).astype(F32)
    row = jnp.floor((site + 0.5) * (1.0 / L))
    x = site - L * row
    z = jnp.floor((row + 0.5) * (1.0 / L))
    y = row - L * z
    for p in range(NMOM):
        turn = (
            mom[p, 0].astype(F32) * x + mom[p, 1].astype(F32) * y + mom[p, 2].astype(F32) * z
        )
        turn = turn - L * jnp.floor((turn + 0.5) * (1.0 / L))
        cosine, sine = sin_cos(turn)
        trig[p : p + 1, :] = cosine
        trig[p + NMOM : p + NMOM + 1, :] = sine
    columns = trig[...].T
    for q in range(2 * NMOM):
        wide_trig[q] = jnp.broadcast_to(columns[:count, q : q + 1], (count, 128))
    phased[depth:, :] = jnp.zeros((padded - depth, 2 * NVEC), BF16)
    waited = 0
    for first in range(0, padded, 128):
        rows = min(128, depth - first)
        while waited < 3 and first + rows > waited * count:
            loads[waited].wait()
            waited += 1
        for part in range(2):
            block = vbuf[part, first : first + rows, :]
            if rows < 128:
                block = jnp.concatenate([block, jnp.zeros((128 - rows, NVEC), BF16)], axis=0)
            flipped[part * NVEC : (part + 1) * NVEC, first : first + 128] = block.T
    for p in range(NMOM):
        for colour in range(3):
            rows = slice(colour * count, (colour + 1) * count)
            for half in range(2):
                cols = slice(half * 128, (half + 1) * 128)
                real = vbuf[0, rows, cols].astype(F32)
                imag = vbuf[1, rows, cols].astype(F32)
                cosine = wide_trig[p]
                sine = wide_trig[p + NMOM]
                phased[rows, half * 128 : half * 128 + 128] = (cosine * real + sine * imag).astype(BF16)
                phased[rows, NVEC + half * 128 : NVEC + half * 128 + 128] = (
                    cosine * imag - sine * real
                ).astype(BF16)
        product = jnp.dot(flipped[...], phased[...], preferred_element_type=F32)
        acc[2 * p] = product[:NVEC, :NVEC] + product[NVEC:, NVEC:]
        acc[2 * p + 1] = product[:NVEC, NVEC:] - product[NVEC:, :NVEC]
    rows = NVEC // YN
    at_row = lax.broadcasted_iota(jnp.int32, (16, NVEC), 0)
    flat = [moments[k] + NMOM * (slices[k] != near).astype(jnp.int32) for k in range(2)]
    note = jnp.where(at_row == 0, flat[0], flat[1]).astype(F32).astype(BF16)
    stores = []
    for step in (2, 1, 3, 0):
        first = pl.multiple_of((my_y ^ step) * rows, rows)
        buf, out = (kbuf, keep) if step == 0 else (sbuf.at[step - 1], (send1, send2, send3)[step - 1])
        for r in range(2 * NMOM):
            buf[r * rows : (r + 1) * rows, :] = (acc[r, pl.ds(first, rows), :] * SCALE).astype(buf.dtype)
        if step:
            buf[2 * NMOM * rows :, :] = note
        store = pltpu.make_async_copy(buf, out, sems.at[3 + step])
        store.start()
        stores.append(store)
    for store in stores:
        store.wait()


def partial_elementals(turned, source, momenta, slices, moments, vectors):
    depth = vectors.shape[2]
    count = depth // 3
    padded = -(-depth // 256) * 256
    height = 2 * NMOM * NVEC // YN
    hbm = lambda: pl.BlockSpec(memory_space=pltpu.HBM)
    sent = jax.ShapeDtypeStruct((height + 16, NVEC), BF16)
    smem = lambda: pl.BlockSpec(memory_space=pltpu.SMEM)
    return pl.pallas_call(
        functools.partial(elementals_kernel, turned),
        in_specs=[smem(), smem(), smem(), smem(), hbm()],
        out_specs=[hbm(), hbm(), hbm(), hbm()],
        scratch_shapes=[
            pltpu.VMEM((2 * NMOM, NVEC, NVEC), F32),
            pltpu.VMEM((8, -(-count // 128) * 128), F32),
            pltpu.VMEM((2 * NMOM, count, 128), F32),
            pltpu.VMEM((2 * NVEC, padded), BF16),
            pltpu.VMEM((padded, 2 * NVEC), BF16),
            pltpu.VMEM((2, depth, NVEC), BF16),
            pltpu.VMEM((height, NVEC), F32),
            pltpu.VMEM((3, height + 16, NVEC), BF16),
            pltpu.SemaphoreType.DMA((7,)),
        ],
        out_shape=[jax.ShapeDtypeStruct((height, NVEC), F32), sent, sent, sent],
        compiler_params=pltpu.CompilerParams(vmem_limit_bytes=60 * 1024 * 1024),
        name="elementals",
    )(source, momenta, slices, moments, vectors)


def sum_kernel(kept, got1, got2, got3, keep, send1, send2, send3):
    rows = NVEC // YN // ZN
    for step, out in enumerate((keep, send1, send2, send3)):
        for r in range(2 * NMOM):
            first = pl.multiple_of(r * NVEC // YN + (lax.axis_index("site") % ZN ^ step) * rows, rows)
            part = kept[pl.ds(first, rows), :]
            for got in (got1, got2, got3):
                part = part + got[pl.ds(first, rows), :].astype(F32)
            out[r * rows : (r + 1) * rows, :] = part.astype(out.dtype)


def sum_and_split(kept, got):
    height = 2 * NMOM * NVEC // YN // ZN
    piece = lambda dtype: jax.ShapeDtypeStruct((height, NVEC), dtype)
    vmem = lambda: pl.BlockSpec(memory_space=pltpu.VMEM)
    return pl.pallas_call(
        sum_kernel,
        in_specs=[vmem() for _ in range(4)],
        out_specs=[vmem() for _ in range(4)],
        out_shape=[piece(F32), piece(BF16), piece(BF16), piece(BF16)],
        compiler_params=pltpu.CompilerParams(vmem_limit_bytes=6 << 20),
        name="sum_split",
    )(kept, *got)


def flip_kernel(t_ref, out):
    for part in range(2):
        out[0, :, part * NVEC : (part + 1) * NVEC] = t_ref[0, part, 0].T


def transposed(perams):
    count, _, spins, nvec, columns = perams.shape
    return pl.pallas_call(
        flip_kernel,
        grid=(count, spins),
        in_specs=[pl.BlockSpec((1, 2, 1, nvec, columns), lambda k, s: (k, 0, s, 0, 0))],
        out_specs=pl.BlockSpec((1, columns, 2 * nvec), lambda k, s: (k, 0, s)),
        out_shape=jax.ShapeDtypeStruct((count, columns, spins * 2 * nvec), BF16),
        compiler_params=pltpu.CompilerParams(vmem_limit_bytes=8 << 20),
        name="transpose_tau",
    )(perams)


def pick_kernel(idx, p0, p1, p2, p3, *outs):
    for step, out in enumerate(outs):
        for k in range(2):
            for dz, piece in enumerate((p0, p1, p2, p3)):
                out[k, dz] = piece[idx[step, k]]


def pick(idx, pieces):
    rows = NVEC // YN // ZN
    vmem = lambda: pl.BlockSpec(memory_space=pltpu.VMEM)
    piece = jax.ShapeDtypeStruct((2, ZN, 2, rows, NVEC), BF16)
    return pl.pallas_call(
        pick_kernel,
        in_specs=[pl.BlockSpec(memory_space=pltpu.SMEM)] + [vmem() for _ in pieces],
        out_specs=[vmem() for _ in range(4)],
        out_shape=[piece] * 4,
        compiler_params=pltpu.CompilerParams(vmem_limit_bytes=6 << 20),
    )(idx, *pieces)


def first_row(y, z, dy, dz):
    rows = NVEC // YN // ZN
    return pl.multiple_of((y ^ dy) * (ZN * rows) + (z ^ dz) * rows, rows)


def middle_kernel(source, f0, f1, f2, f3, t_ref, tt_ref, out, fmat, gmat):
    k = pl.program_id(0)
    rows = NVEC // YN // ZN
    site = lax.axis_index("site")
    same_half = lax.axis_index("cuts") // 8 == source[0] // 2 // 8
    my_y = site // ZN
    my_z = site % ZN
    far_z = my_z ^ jnp.where(same_half, 0, 2)
    for dy, f_ref in enumerate((f0, f1, f2, f3)):
        for dz in range(ZN):
            first = first_row(my_y, far_z, dy, dz)
            f_re = f_ref[k, dz, 0]
            f_im = f_ref[k, dz, 1]
            fmat[pl.ds(first, rows), :NVEC] = f_re
            fmat[pl.ds(first, rows), NVEC:] = -f_im
            fmat[pl.ds(NVEC + first, rows), :NVEC] = f_im
            fmat[pl.ds(NVEC + first, rows), NVEC:] = f_re
    wide = t_ref.shape[-1]
    f_all = fmat[...]
    for spin in range(4):
        tau = t_ref[0, :, spin].reshape(2 * NVEC, wide)
        left = jnp.dot(f_all, tau, preferred_element_type=F32).astype(BF16)
        home = (spin + 2) % 4
        if home >= 2:
            left = -left
        base = home * 2 * NVEC
        gmat[base : base + NVEC, :wide] = left[:NVEC]
        gmat[base + NVEC : base + 2 * NVEC, :wide] = left[NVEC:]
        gmat[base : base + NVEC, wide:] = left[NVEC:]
        gmat[base + NVEC : base + 2 * NVEC, wide:] = -left[:NVEC]
    out[0] = jnp.dot(tt_ref[0], gmat[...], preferred_element_type=F32).astype(BF16)


def middle_of(source_slice, source, perams, perams_t):
    count, _, spins, nvec, wide = perams.shape
    rows = NVEC // YN // ZN
    f_spec = lambda: pl.BlockSpec((count, ZN, 2, rows, NVEC), lambda k, *_: (0, 0, 0, 0, 0))
    return pl.pallas_call(
        middle_kernel,
        grid_spec=pltpu.PrefetchScalarGridSpec(
            num_scalar_prefetch=1,
            grid=(count,),
            in_specs=[f_spec() for _ in range(4)]
            + [
                pl.BlockSpec((1, 2, spins, nvec, wide), lambda k, *_: (k, 0, 0, 0, 0)),
                pl.BlockSpec((1, wide, spins * 2 * nvec), lambda k, *_: (k, 0, 0)),
            ],
            out_specs=pl.BlockSpec((1, wide, 2 * wide), lambda k, *_: (k, 0, 0)),
            scratch_shapes=[
                pltpu.VMEM((2 * NVEC, 2 * NVEC), BF16),
                pltpu.VMEM((spins * 2 * nvec, 2 * wide), BF16),
            ],
        ),
        out_shape=jax.ShapeDtypeStruct((count, wide, 2 * wide), BF16),
        compiler_params=pltpu.CompilerParams(vmem_limit_bytes=36 << 20),
        name="middle",
    )(source_slice, *source, perams, perams_t)


def table_at(row, column):
    shared = row & column
    return jnp.where(((shared & 1) ^ (shared >> 1)) == 1, -0.5, 0.5)


def outer_kernel(order, s0, s1, s2, s3, m_ref, out, smat):
    k = pl.program_id(0)
    rows = NVEC // YN // ZN
    site = lax.axis_index("site")
    my_y = site // ZN
    my_z = site % ZN
    for dy, s_ref in enumerate((s0, s1, s2, s3)):
        for dz in range(ZN):
            first = first_row(my_y, my_z, dy, dz)
            s_re = s_ref[k, dz, 0]
            s_im = s_ref[k, dz, 1]
            smat[pl.ds(first, rows), :NVEC] = s_re
            smat[pl.ds(first, rows), NVEC:] = s_im
            smat[pl.ds(NVEC + first, rows), :NVEC] = -s_im
            smat[pl.ds(NVEC + first, rows), NVEC:] = s_re
    wide = m_ref.shape[1]
    s_all = smat[...]
    inner = []
    for e in range(2):
        block = jnp.concatenate(
            [
                m_ref[0, :, e * NVEC : (e + 1) * NVEC],
                m_ref[0, :, wide + e * NVEC : wide + (e + 1) * NVEC],
            ],
            axis=1,
        )
        inner.append(jnp.dot(block, s_all, preferred_element_type=F32))
    for f in range(2):
        mixed = inner[0] * table_at(order[0], order[f]) + inner[1] * table_at(order[1], order[f])
        out[0, 0, :, f * NVEC : (f + 1) * NVEC] = mixed[:, :NVEC].astype(BF16)
        out[0, 1, :, f * NVEC : (f + 1) * NVEC] = mixed[:, NVEC:].astype(BF16)


def correlators_of(spin_order, sinks, middle):
    count, wide, _ = middle.shape
    rows = NVEC // YN // ZN
    s_spec = lambda: pl.BlockSpec((count, ZN, 2, rows, NVEC), lambda k, *_: (0, 0, 0, 0, 0))
    return pl.pallas_call(
        outer_kernel,
        grid_spec=pltpu.PrefetchScalarGridSpec(
            num_scalar_prefetch=1,
            grid=(count,),
            in_specs=[s_spec() for _ in range(4)]
            + [pl.BlockSpec((1, wide, 2 * wide), lambda k, *_: (k, 0, 0))],
            out_specs=pl.BlockSpec((1, 2, wide, wide), lambda k, *_: (k, 0, 0, 0)),
            scratch_shapes=[pltpu.VMEM((2 * NVEC, 2 * NVEC), BF16)],
        ),
        out_shape=jax.ShapeDtypeStruct((count, 2, wide, wide), BF16),
        compiler_params=pltpu.CompilerParams(vmem_limit_bytes=16 << 20),
        name="outer",
    )(spin_order, *sinks, middle)


def body(
    eigen_vectors, perambulators, momenta, source_slice, sink_slices, sink_momenta, spin_order
):
    slab_slices = eigen_vectors.shape[0]
    site_count = eigen_vectors.shape[-1]
    cut = lax.axis_index("cuts")
    source = source_slice[0]
    root = source // slab_slices
    near = source % slab_slices
    root_h = root // 8
    root_x = root // 2 % 4
    flat = (sink_slices != near).astype(jnp.int32) * NMOM + sink_momenta
    vectors = eigen_vectors.swapaxes(3, 4).reshape(slab_slices, 2, 3 * site_count, NVEC)

    def swap_y(parts):
        got = {}
        for step in (2, 1, 3):
            got[step] = lax.ppermute(parts[step], "site", y_swap(step))
        return [got[1], got[2], got[3]]

    def swap_z(parts):
        return [lax.ppermute(parts[step], "site", z_swap(step)) for step in (1, 2, 3)]

    def reduce_slice(turned):
        parts = partial_elementals(
            turned, source_slice, momenta, sink_slices, sink_momenta, vectors
        )
        got = swap_y(parts)
        notes = got
        parts = sum_and_split(parts[0], got)
        got = swap_z(parts)
        chunk = (parts[0] + sum(g.astype(F32) for g in got)).astype(BF16)
        return chunk.reshape(NMOM, 2, NVEC // YN // ZN, NVEC), notes

    chunk_a, notes = reduce_slice(False)
    chunk_b, _ = reduce_slice(True)
    tall = 2 * NMOM * NVEC // YN
    idx = jnp.stack([flat] + [v[tall : tall + 2, 0].astype(jnp.int32) for v in notes])

    held = chunk_a
    my_x = cut // 2 % 4
    for step in (1, 2, 3):
        got = lax.ppermute(chunk_a, "cuts", cut_swap(step, 0))
        held = jnp.where((my_x ^ step) == root_x, got, held)
    got = lax.ppermute(held, ("site", "cuts"), half_swap())
    held = jnp.where(cut // 8 == root_h, held, got)
    got = lax.ppermute(held, "cuts", cut_swap(0, 1))
    held = jnp.where(cut % 2 == root % 2, held, got)

    pieces = [held] + swap_z([held] * 4)
    parts = pick(idx % NMOM, pieces)
    source_parts = [parts[0]] + swap_y(parts)
    own_ab = jnp.concatenate([chunk_a, chunk_b], axis=0)
    pieces = [own_ab] + swap_z([own_ab] * 4)
    pieces, _ = lax.optimization_barrier((pieces, parts))
    parts = pick(idx, pieces)
    sink_parts = [parts[0]] + swap_y(parts)

    count = perambulators.shape[0]
    perams = perambulators.reshape(count, 2, 4, NVEC, 2 * NVEC)
    perams_t = transposed(perams)
    middle = middle_of(source_slice, source_parts, perams, perams_t)
    return correlators_of(spin_order, sink_parts, middle)


def solution(mesh):
    placed = (
        P("cuts", None, None, None, "site"),
        P(("site", "cuts"), None, None, None),
        P(),
        P(),
        P(("site", "cuts")),
        P(("site", "cuts")),
        P(),
    )
    return jax.shard_map(
        body,
        mesh=mesh,
        in_specs=placed,
        out_specs=P(("site", "cuts"), None, None, None),
        check_vma=False,
    )
```

```python
import functools
import math

import jax
import jax.numpy as jnp
from jax import lax
from jax.experimental import pallas as pl
from jax.experimental.pallas import tpu as pltpu
from jax.sharding import PartitionSpec as P


L = 96
PLANES = 1
NMOM = 3
NVEC = 256
YN = 4
ZN = 4
SCALE = 1.0 / math.sqrt(6.0 * L * L * PLANES)
F32 = jnp.float32
BF16 = jnp.bfloat16


def y_swap(step):
    return [(y * ZN + z, (y ^ step) * ZN + z) for y in range(YN) for z in range(ZN)]


def z_swap(step):
    return [(y * ZN + z, y * ZN + (z ^ step)) for y in range(YN) for z in range(ZN)]


def cut_swap(dx, dc):
    return [
        (h * 8 + x * 2 + c, h * 8 + (x ^ dx) * 2 + (c ^ dc))
        for h in range(2)
        for x in range(4)
        for c in range(2)
    ]


def half_swap():
    return [
        ((y * ZN + z) * 16 + h * 8 + rest, (y * ZN + (z ^ 2)) * 16 + (h ^ 1) * 8 + rest)
        for y in range(YN)
        for z in range(ZN)
        for h in range(2)
        for rest in range(8)
    ]


def sin_cos(winding):
    quarter = jnp.floor((winding + 12.5) * (1.0 / 24.0))
    angle = (winding - 24.0 * quarter) * (2.0 * math.pi / L)
    sq = angle * angle
    sine = angle * (1.0 + sq * (-1 / 6 + sq * (1 / 120 + sq * (-1 / 5040 + sq * (1 / 362880)))))
    cosine = 1.0 + sq * (
        -1 / 2 + sq * (1 / 24 + sq * (-1 / 720 + sq * (1 / 40320 + sq * (-1 / 3628800))))
    )
    odd = (quarter == 1.0) | (quarter == 3.0)
    cos_out = jnp.where(odd, sine, cosine)
    sin_out = jnp.where(odd, cosine, sine)
    cos_out = jnp.where((quarter == 1.0) | (quarter == 2.0), -cos_out, cos_out)
    sin_out = jnp.where((quarter == 2.0) | (quarter == 3.0), -sin_out, sin_out)
    return cos_out, sin_out


def scalar_row(source, turned):
    near = source[0] % 2
    return near, (1 - near if turned else near)


def elementals_kernel(
    turned, source, mom, slices, moments, v_hbm, keep, send1, send2, send3, acc, trig, wide_trig, flipped, phased, vbuf, kbuf, sbuf, sems
):
    depth = vbuf.shape[1]
    count = depth // 3
    padded = flipped.shape[1]
    span = trig.shape[1]
    near, mine = scalar_row(source, turned)
    place = lax.axis_index("site")
    my_y = place // ZN
    loads = []
    for colour in range(3):
        rows = pl.ds(colour * count, count)
        load = pltpu.make_async_copy(
            v_hbm.at[mine, :, rows, :], vbuf.at[:, rows, :], sems.at[colour]
        )
        load.start()
        loads.append(load)
    site = (place * count + lax.broadcasted_iota(jnp.int32, (1, span), 1)).astype(F32)
    row = jnp.floor((site + 0.5) * (1.0 / L))
    x = site - L * row
    z = jnp.floor((row + 0.5) * (1.0 / L))
    y = row - L * z
    for p in range(NMOM):
        turn = (
            mom[p, 0].astype(F32) * x + mom[p, 1].astype(F32) * y + mom[p, 2].astype(F32) * z
        )
        turn = turn - L * jnp.floor((turn + 0.5) * (1.0 / L))
        cosine, sine = sin_cos(turn)
        trig[p : p + 1, :] = cosine
        trig[p + NMOM : p + NMOM + 1, :] = sine
    columns = trig[...].T
    for q in range(2 * NMOM):
        wide_trig[q] = jnp.broadcast_to(columns[:count, q : q + 1], (count, 128))
    phased[:, depth:, :] = jnp.zeros((NMOM, padded - depth, 2 * NVEC), BF16)
    waited = 0
    for first in range(0, padded, 128):
        rows = min(128, depth - first)
        while waited < 3 and first + rows > waited * count:
            loads[waited].wait()
            waited += 1
        for part in range(2):
            block = vbuf[part, first : first + rows, :]
            if rows < 128:
                block = jnp.concatenate([block, jnp.zeros((128 - rows, NVEC), BF16)], axis=0)
            flipped[part * NVEC : (part + 1) * NVEC, first : first + 128] = block.T
    for p in range(NMOM):
        for colour in range(3):
            rows = slice(colour * count, (colour + 1) * count)
            for half in range(2):
                cols = slice(half * 128, (half + 1) * 128)
                real = vbuf[0, rows, cols].astype(F32)
                imag = vbuf[1, rows, cols].astype(F32)
                cosine = wide_trig[p]
                sine = wide_trig[p + NMOM]
                phased[p, rows, half * 128 : half * 128 + 128] = (cosine * real + sine * imag).astype(BF16)
                phased[p, rows, NVEC + half * 128 : NVEC + half * 128 + 128] = (
                    cosine * imag - sine * real
                ).astype(BF16)
        product = jnp.dot(flipped[...], phased[p], preferred_element_type=F32)
        acc[2 * p] = product[:NVEC, :NVEC] + product[NVEC:, NVEC:]
        acc[2 * p + 1] = product[:NVEC, NVEC:] - product[NVEC:, :NVEC]
    rows = NVEC // YN
    at_row = lax.broadcasted_iota(jnp.int32, (16, NVEC), 0)
    flat = [moments[k] + NMOM * (slices[k] != near).astype(jnp.int32) for k in range(2)]
    note = jnp.where(at_row == 0, flat[0], flat[1]).astype(F32).astype(BF16)
    stores = []
    for step in (2, 1, 3, 0):
        first = pl.multiple_of((my_y ^ step) * rows, rows)
        buf, out = (kbuf, keep) if step == 0 else (sbuf.at[step - 1], (send1, send2, send3)[step - 1])
        for r in range(2 * NMOM):
            buf[r * rows : (r + 1) * rows, :] = (acc[r, pl.ds(first, rows), :] * SCALE).astype(buf.dtype)
        if step:
            buf[2 * NMOM * rows :, :] = note
        store = pltpu.make_async_copy(buf, out, sems.at[3 + step])
        store.start()
        stores.append(store)
    for store in stores:
        store.wait()


def partial_elementals(turned, source, momenta, slices, moments, vectors):
    depth = vectors.shape[2]
    count = depth // 3
    padded = -(-depth // 256) * 256
    height = 2 * NMOM * NVEC // YN
    hbm = lambda: pl.BlockSpec(memory_space=pltpu.HBM)
    sent = jax.ShapeDtypeStruct((height + 16, NVEC), BF16)
    smem = lambda: pl.BlockSpec(memory_space=pltpu.SMEM)
    return pl.pallas_call(
        functools.partial(elementals_kernel, turned),
        in_specs=[smem(), smem(), smem(), smem(), hbm()],
        out_specs=[hbm(), hbm(), hbm(), hbm()],
        scratch_shapes=[
            pltpu.VMEM((2 * NMOM, NVEC, NVEC), F32),
            pltpu.VMEM((8, -(-count // 128) * 128), F32),
            pltpu.VMEM((2 * NMOM, count, 128), F32),
            pltpu.VMEM((2 * NVEC, padded), BF16),
            pltpu.VMEM((NMOM, padded, 2 * NVEC), BF16),
            pltpu.VMEM((2, depth, NVEC), BF16),
            pltpu.VMEM((height, NVEC), F32),
            pltpu.VMEM((3, height + 16, NVEC), BF16),
            pltpu.SemaphoreType.DMA((7,)),
        ],
        out_shape=[jax.ShapeDtypeStruct((height, NVEC), F32), sent, sent, sent],
        compiler_params=pltpu.CompilerParams(vmem_limit_bytes=60 * 1024 * 1024),
        name="elementals",
    )(source, momenta, slices, moments, vectors)


def sum_kernel(kept, got1, got2, got3, keep, send1, send2, send3):
    rows = NVEC // YN // ZN
    for step, out in enumerate((keep, send1, send2, send3)):
        for r in range(2 * NMOM):
            first = pl.multiple_of(r * NVEC // YN + (lax.axis_index("site") % ZN ^ step) * rows, rows)
            part = kept[pl.ds(first, rows), :]
            for got in (got1, got2, got3):
                part = part + got[pl.ds(first, rows), :].astype(F32)
            out[r * rows : (r + 1) * rows, :] = part.astype(out.dtype)


def sum_and_split(kept, got):
    height = 2 * NMOM * NVEC // YN // ZN
    piece = lambda dtype: jax.ShapeDtypeStruct((height, NVEC), dtype)
    vmem = lambda: pl.BlockSpec(memory_space=pltpu.VMEM)
    return pl.pallas_call(
        sum_kernel,
        in_specs=[vmem() for _ in range(4)],
        out_specs=[vmem() for _ in range(4)],
        out_shape=[piece(F32), piece(BF16), piece(BF16), piece(BF16)],
        compiler_params=pltpu.CompilerParams(vmem_limit_bytes=6 << 20),
        name="sum_split",
    )(kept, *got)


def flip_kernel(t_ref, out):
    for part in range(2):
        out[0, :, part * NVEC : (part + 1) * NVEC] = t_ref[0, part, 0].T


def transposed(perams):
    count, _, spins, nvec, columns = perams.shape
    return pl.pallas_call(
        flip_kernel,
        grid=(count, spins),
        in_specs=[pl.BlockSpec((1, 2, 1, nvec, columns), lambda k, s: (k, 0, s, 0, 0))],
        out_specs=pl.BlockSpec((1, columns, 2 * nvec), lambda k, s: (k, 0, s)),
        out_shape=jax.ShapeDtypeStruct((count, columns, spins * 2 * nvec), BF16),
        compiler_params=pltpu.CompilerParams(vmem_limit_bytes=8 << 20),
        name="transpose_tau",
    )(perams)


def pick_kernel(idx, p0, p1, p2, p3, *outs):
    for step, out in enumerate(outs):
        for k in range(2):
            for dz, piece in enumerate((p0, p1, p2, p3)):
                out[k, dz] = piece[idx[step, k]]


def pick(idx, pieces):
    rows = NVEC // YN // ZN
    vmem = lambda: pl.BlockSpec(memory_space=pltpu.VMEM)
    piece = jax.ShapeDtypeStruct((2, ZN, 2, rows, NVEC), BF16)
    return pl.pallas_call(
        pick_kernel,
        in_specs=[pl.BlockSpec(memory_space=pltpu.SMEM)] + [vmem() for _ in pieces],
        out_specs=[vmem() for _ in range(4)],
        out_shape=[piece] * 4,
        compiler_params=pltpu.CompilerParams(vmem_limit_bytes=6 << 20),
    )(idx, *pieces)


def first_row(y, z, dy, dz):
    rows = NVEC // YN // ZN
    return pl.multiple_of((y ^ dy) * (ZN * rows) + (z ^ dz) * rows, rows)


def middle_kernel(source, f0, f1, f2, f3, t_ref, tt_ref, out, fmat, gmat):
    k = pl.program_id(0)
    rows = NVEC // YN // ZN
    site = lax.axis_index("site")
    same_half = lax.axis_index("cuts") // 8 == source[0] // 2 // 8
    my_y = site // ZN
    my_z = site % ZN
    far_z = my_z ^ jnp.where(same_half, 0, 2)
    for dy, f_ref in enumerate((f0, f1, f2, f3)):
        for dz in range(ZN):
            first = first_row(my_y, far_z, dy, dz)
            f_re = f_ref[k, dz, 0]
            f_im = f_ref[k, dz, 1]
            fmat[pl.ds(first, rows), :NVEC] = f_re
            fmat[pl.ds(first, rows), NVEC:] = -f_im
            fmat[pl.ds(NVEC + first, rows), :NVEC] = f_im
            fmat[pl.ds(NVEC + first, rows), NVEC:] = f_re
    wide = t_ref.shape[-1]
    f_all = fmat[...]
    for spin in range(4):
        tau = t_ref[0, :, spin].reshape(2 * NVEC, wide)
        left = jnp.dot(f_all, tau, preferred_element_type=F32).astype(BF16)
        home = (spin + 2) % 4
        if home >= 2:
            left = -left
        base = home * 2 * NVEC
        gmat[base : base + NVEC, :wide] = left[:NVEC]
        gmat[base + NVEC : base + 2 * NVEC, :wide] = left[NVEC:]
        gmat[base : base + NVEC, wide:] = left[NVEC:]
        gmat[base + NVEC : base + 2 * NVEC, wide:] = -left[:NVEC]
    out[0] = jnp.dot(tt_ref[0], gmat[...], preferred_element_type=F32).astype(BF16)


def middle_of(source_slice, source, perams, perams_t):
    count, _, spins, nvec, wide = perams.shape
    rows = NVEC // YN // ZN
    f_spec = lambda: pl.BlockSpec((count, ZN, 2, rows, NVEC), lambda k, *_: (0, 0, 0, 0, 0))
    return pl.pallas_call(
        middle_kernel,
        grid_spec=pltpu.PrefetchScalarGridSpec(
            num_scalar_prefetch=1,
            grid=(count,),
            in_specs=[f_spec() for _ in range(4)]
            + [
                pl.BlockSpec((1, 2, spins, nvec, wide), lambda k, *_: (k, 0, 0, 0, 0)),
                pl.BlockSpec((1, wide, spins * 2 * nvec), lambda k, *_: (k, 0, 0)),
            ],
            out_specs=pl.BlockSpec((1, wide, 2 * wide), lambda k, *_: (k, 0, 0)),
            scratch_shapes=[
                pltpu.VMEM((2 * NVEC, 2 * NVEC), BF16),
                pltpu.VMEM((spins * 2 * nvec, 2 * wide), BF16),
            ],
        ),
        out_shape=jax.ShapeDtypeStruct((count, wide, 2 * wide), BF16),
        compiler_params=pltpu.CompilerParams(vmem_limit_bytes=36 << 20),
        name="middle",
    )(source_slice, *source, perams, perams_t)


def table_at(row, column):
    shared = row & column
    return jnp.where(((shared & 1) ^ (shared >> 1)) == 1, -0.5, 0.5)


def outer_kernel(order, s0, s1, s2, s3, m_ref, out, smat):
    k = pl.program_id(0)
    rows = NVEC // YN // ZN
    site = lax.axis_index("site")
    my_y = site // ZN
    my_z = site % ZN
    for dy, s_ref in enumerate((s0, s1, s2, s3)):
        for dz in range(ZN):
            first = first_row(my_y, my_z, dy, dz)
            s_re = s_ref[k, dz, 0]
            s_im = s_ref[k, dz, 1]
            smat[pl.ds(first, rows), :NVEC] = s_re
            smat[pl.ds(first, rows), NVEC:] = s_im
            smat[pl.ds(NVEC + first, rows), :NVEC] = -s_im
            smat[pl.ds(NVEC + first, rows), NVEC:] = s_re
    wide = m_ref.shape[1]
    s_all = smat[...]
    inner = []
    for e in range(2):
        block = jnp.concatenate(
            [
                m_ref[0, :, e * NVEC : (e + 1) * NVEC],
                m_ref[0, :, wide + e * NVEC : wide + (e + 1) * NVEC],
            ],
            axis=1,
        )
        inner.append(jnp.dot(block, s_all, preferred_element_type=F32))
    for f in range(2):
        mixed = inner[0] * table_at(order[0], order[f]) + inner[1] * table_at(order[1], order[f])
        out[0, 0, :, f * NVEC : (f + 1) * NVEC] = mixed[:, :NVEC].astype(BF16)
        out[0, 1, :, f * NVEC : (f + 1) * NVEC] = mixed[:, NVEC:].astype(BF16)


def correlators_of(spin_order, sinks, middle):
    count, wide, _ = middle.shape
    rows = NVEC // YN // ZN
    s_spec = lambda: pl.BlockSpec((count, ZN, 2, rows, NVEC), lambda k, *_: (0, 0, 0, 0, 0))
    return pl.pallas_call(
        outer_kernel,
        grid_spec=pltpu.PrefetchScalarGridSpec(
            num_scalar_prefetch=1,
            grid=(count,),
            in_specs=[s_spec() for _ in range(4)]
            + [pl.BlockSpec((1, wide, 2 * wide), lambda k, *_: (k, 0, 0))],
            out_specs=pl.BlockSpec((1, 2, wide, wide), lambda k, *_: (k, 0, 0, 0)),
            scratch_shapes=[pltpu.VMEM((2 * NVEC, 2 * NVEC), BF16)],
        ),
        out_shape=jax.ShapeDtypeStruct((count, 2, wide, wide), BF16),
        compiler_params=pltpu.CompilerParams(vmem_limit_bytes=16 << 20),
        name="outer",
    )(spin_order, *sinks, middle)


def body(
    eigen_vectors, perambulators, momenta, source_slice, sink_slices, sink_momenta, spin_order
):
    slab_slices = eigen_vectors.shape[0]
    site_count = eigen_vectors.shape[-1]
    cut = lax.axis_index("cuts")
    source = source_slice[0]
    root = source // slab_slices
    near = source % slab_slices
    root_h = root // 8
    root_x = root // 2 % 4
    flat = (sink_slices != near).astype(jnp.int32) * NMOM + sink_momenta
    vectors = eigen_vectors.swapaxes(3, 4).reshape(slab_slices, 2, 3 * site_count, NVEC)

    def swap_y(parts):
        got = {}
        for step in (2, 1, 3):
            got[step] = lax.ppermute(parts[step], "site", y_swap(step))
        return [got[1], got[2], got[3]]

    def swap_z(parts):
        return [lax.ppermute(parts[step], "site", z_swap(step)) for step in (1, 2, 3)]

    def reduce_slice(turned):
        parts = partial_elementals(
            turned, source_slice, momenta, sink_slices, sink_momenta, vectors
        )
        got = swap_y(parts)
        notes = got
        parts = sum_and_split(parts[0], got)
        got = swap_z(parts)
        chunk = (parts[0] + sum(g.astype(F32) for g in got)).astype(BF16)
        return chunk.reshape(NMOM, 2, NVEC // YN // ZN, NVEC), notes

    chunk_a, notes = reduce_slice(False)
    chunk_b, _ = reduce_slice(True)
    tall = 2 * NMOM * NVEC // YN
    idx = jnp.stack([flat] + [v[tall : tall + 2, 0].astype(jnp.int32) for v in notes])

    held = chunk_a
    my_x = cut // 2 % 4
    for step in (1, 2, 3):
        got = lax.ppermute(chunk_a, "cuts", cut_swap(step, 0))
        held = jnp.where((my_x ^ step) == root_x, got, held)
    got = lax.ppermute(held, ("site", "cuts"), half_swap())
    held = jnp.where(cut // 8 == root_h, held, got)
    got = lax.ppermute(held, "cuts", cut_swap(0, 1))
    held = jnp.where(cut % 2 == root % 2, held, got)

    pieces = [held] + swap_z([held] * 4)
    parts = pick(idx % NMOM, pieces)
    source_parts = [parts[0]] + swap_y(parts)
    own_ab = jnp.concatenate([chunk_a, chunk_b], axis=0)
    pieces = [own_ab] + swap_z([own_ab] * 4)
    pieces, _ = lax.optimization_barrier((pieces, parts))
    parts = pick(idx, pieces)
    sink_parts = [parts[0]] + swap_y(parts)

    count = perambulators.shape[0]
    perams = perambulators.reshape(count, 2, 4, NVEC, 2 * NVEC)
    perams_t = transposed(perams)
    middle = middle_of(source_slice, source_parts, perams, perams_t)
    return correlators_of(spin_order, sink_parts, middle)


def solution(mesh):
    placed = (
        P("cuts", None, None, None, "site"),
        P(("site", "cuts"), None, None, None),
        P(),
        P(),
        P(("site", "cuts")),
        P(("site", "cuts")),
        P(),
    )
    return jax.shard_map(
        body,
        mesh=mesh,
        in_specs=placed,
        out_specs=P(("site", "cuts"), None, None, None),
        check_vma=False,
    )
```

```python
import functools
import math

import jax
import jax.numpy as jnp
from jax import lax
from jax.experimental import pallas as pl
from jax.experimental.pallas import tpu as pltpu
from jax.sharding import PartitionSpec as P


L = 96
PLANES = 1
NMOM = 3
NVEC = 256
YN = 4
ZN = 4
SCALE = 1.0 / math.sqrt(6.0 * L * L * PLANES)
F32 = jnp.float32
BF16 = jnp.bfloat16


def y_swap(step):
    return [(y * ZN + z, (y ^ step) * ZN + z) for y in range(YN) for z in range(ZN)]


def z_swap(step):
    return [(y * ZN + z, y * ZN + (z ^ step)) for y in range(YN) for z in range(ZN)]


def cut_swap(dx, dc):
    return [
        (h * 8 + x * 2 + c, h * 8 + (x ^ dx) * 2 + (c ^ dc))
        for h in range(2)
        for x in range(4)
        for c in range(2)
    ]


def half_swap():
    return [
        ((y * ZN + z) * 16 + h * 8 + rest, (y * ZN + (z ^ 2)) * 16 + (h ^ 1) * 8 + rest)
        for y in range(YN)
        for z in range(ZN)
        for h in range(2)
        for rest in range(8)
    ]


def sin_cos(winding):
    quarter = jnp.floor((winding + 12.5) * (1.0 / 24.0))
    angle = (winding - 24.0 * quarter) * (2.0 * math.pi / L)
    sq = angle * angle
    sine = angle * (1.0 + sq * (-1 / 6 + sq * (1 / 120 + sq * (-1 / 5040 + sq * (1 / 362880)))))
    cosine = 1.0 + sq * (
        -1 / 2 + sq * (1 / 24 + sq * (-1 / 720 + sq * (1 / 40320 + sq * (-1 / 3628800))))
    )
    odd = (quarter == 1.0) | (quarter == 3.0)
    cos_out = jnp.where(odd, sine, cosine)
    sin_out = jnp.where(odd, cosine, sine)
    cos_out = jnp.where((quarter == 1.0) | (quarter == 2.0), -cos_out, cos_out)
    sin_out = jnp.where((quarter == 2.0) | (quarter == 3.0), -sin_out, sin_out)
    return cos_out, sin_out


def scalar_row(source, turned):
    near = source[0] % 2
    return near, (1 - near if turned else near)


def elementals_kernel(
    turned, source, mom, slices, moments, v_hbm, keep, send1, send2, send3, acc, trig, wide_trig, flipped, phased, vbuf, kbuf, sbuf, sems
):
    depth = vbuf.shape[1]
    count = depth // 3
    padded = flipped.shape[1]
    span = trig.shape[1]
    near, mine = scalar_row(source, turned)
    place = lax.axis_index("site")
    my_y = place // ZN
    loads = []
    for colour in range(3):
        rows = pl.ds(colour * count, count)
        load = pltpu.make_async_copy(
            v_hbm.at[mine, :, rows, :], vbuf.at[:, rows, :], sems.at[colour]
        )
        load.start()
        loads.append(load)
    site = (place * count + lax.broadcasted_iota(jnp.int32, (1, span), 1)).astype(F32)
    row = jnp.floor((site + 0.5) * (1.0 / L))
    x = site - L * row
    z = jnp.floor((row + 0.5) * (1.0 / L))
    y = row - L * z
    for p in range(NMOM):
        turn = (
            mom[p, 0].astype(F32) * x + mom[p, 1].astype(F32) * y + mom[p, 2].astype(F32) * z
        )
        turn = turn - L * jnp.floor((turn + 0.5) * (1.0 / L))
        cosine, sine = sin_cos(turn)
        trig[p : p + 1, :] = cosine
        trig[p + NMOM : p + NMOM + 1, :] = sine
    columns = trig[...].T
    for q in range(2 * NMOM):
        wide_trig[q] = jnp.broadcast_to(columns[:count, q : q + 1], (count, 128))
    phased[:, depth:, :] = jnp.zeros((NMOM, padded - depth, 2 * NVEC), BF16)
    waited = 0
    for first in range(0, padded, 128):
        rows = min(128, depth - first)
        while waited < 3 and first + rows > waited * count:
            loads[waited].wait()
            waited += 1
        for part in range(2):
            block = vbuf[part, first : first + rows, :]
            if rows < 128:
                block = jnp.concatenate([block, jnp.zeros((128 - rows, NVEC), BF16)], axis=0)
            flipped[part * NVEC : (part + 1) * NVEC, first : first + 128] = block.T
    for p in range(NMOM):
        for colour in range(3):
            rows = slice(colour * count, (colour + 1) * count)
            for half in range(2):
                cols = slice(half * 128, (half + 1) * 128)
                real = vbuf[0, rows, cols].astype(F32)
                imag = vbuf[1, rows, cols].astype(F32)
                cosine = wide_trig[p]
                sine = wide_trig[p + NMOM]
                phased[p, rows, half * 128 : half * 128 + 128] = (cosine * real + sine * imag).astype(BF16)
                phased[p, rows, NVEC + half * 128 : NVEC + half * 128 + 128] = (
                    cosine * imag - sine * real
                ).astype(BF16)
        product = jnp.dot(flipped[...], phased[p], preferred_element_type=F32)
        acc[2 * p] = product[:NVEC, :NVEC] + product[NVEC:, NVEC:]
        acc[2 * p + 1] = product[:NVEC, NVEC:] - product[NVEC:, :NVEC]
    rows = NVEC // YN
    at_row = lax.broadcasted_iota(jnp.int32, (16, NVEC), 0)
    flat = [moments[k] + NMOM * (slices[k] != near).astype(jnp.int32) for k in range(2)]
    note = jnp.where(at_row == 0, flat[0], flat[1]).astype(F32).astype(BF16)
    stores = []
    for step in (2, 1, 3, 0):
        first = pl.multiple_of((my_y ^ step) * rows, rows)
        buf, out = (kbuf, keep) if step == 0 else (sbuf.at[step - 1], (send1, send2, send3)[step - 1])
        for r in range(2 * NMOM):
            buf[r * rows : (r + 1) * rows, :] = (acc[r, pl.ds(first, rows), :] * SCALE).astype(buf.dtype)
        if step:
            buf[2 * NMOM * rows :, :] = note
        store = pltpu.make_async_copy(buf, out, sems.at[3 + step])
        store.start()
        stores.append(store)
    for store in stores:
        store.wait()


def partial_elementals(turned, source, momenta, slices, moments, vectors):
    depth = vectors.shape[2]
    count = depth // 3
    padded = -(-depth // 256) * 256
    height = 2 * NMOM * NVEC // YN
    hbm = lambda: pl.BlockSpec(memory_space=pltpu.HBM)
    sent = jax.ShapeDtypeStruct((height + 16, NVEC), BF16)
    smem = lambda: pl.BlockSpec(memory_space=pltpu.SMEM)
    return pl.pallas_call(
        functools.partial(elementals_kernel, turned),
        in_specs=[smem(), smem(), smem(), smem(), hbm()],
        out_specs=[hbm(), hbm(), hbm(), hbm()],
        scratch_shapes=[
            pltpu.VMEM((2 * NMOM, NVEC, NVEC), F32),
            pltpu.VMEM((8, -(-count // 128) * 128), F32),
            pltpu.VMEM((2 * NMOM, count, 128), F32),
            pltpu.VMEM((2 * NVEC, padded), BF16),
            pltpu.VMEM((NMOM, padded, 2 * NVEC), BF16),
            pltpu.VMEM((2, depth, NVEC), BF16),
            pltpu.VMEM((height, NVEC), F32),
            pltpu.VMEM((3, height + 16, NVEC), BF16),
            pltpu.SemaphoreType.DMA((7,)),
        ],
        out_shape=[jax.ShapeDtypeStruct((height, NVEC), F32), sent, sent, sent],
        compiler_params=pltpu.CompilerParams(vmem_limit_bytes=60 * 1024 * 1024),
        name="elementals",
    )(source, momenta, slices, moments, vectors)


def sum_kernel(kept, got1, got2, got3, keep, send1, send2, send3):
    rows = NVEC // YN // ZN
    for step, out in enumerate((keep, send1, send2, send3)):
        for r in range(2 * NMOM):
            first = pl.multiple_of(r * NVEC // YN + (lax.axis_index("site") % ZN ^ step) * rows, rows)
            part = kept[pl.ds(first, rows), :]
            for got in (got1, got2, got3):
                part = part + got[pl.ds(first, rows), :].astype(F32)
            out[r * rows : (r + 1) * rows, :] = part.astype(out.dtype)


def sum_and_split(kept, got):
    height = 2 * NMOM * NVEC // YN // ZN
    piece = lambda dtype: jax.ShapeDtypeStruct((height, NVEC), dtype)
    vmem = lambda: pl.BlockSpec(memory_space=pltpu.VMEM)
    return pl.pallas_call(
        sum_kernel,
        in_specs=[vmem() for _ in range(4)],
        out_specs=[vmem() for _ in range(4)],
        out_shape=[piece(F32), piece(BF16), piece(BF16), piece(BF16)],
        compiler_params=pltpu.CompilerParams(vmem_limit_bytes=6 << 20),
        name="sum_split",
    )(kept, *got)


def flip_kernel(t_ref, out):
    for part in range(2):
        out[0, :, part * NVEC : (part + 1) * NVEC] = t_ref[0, part, 0].T


def transposed(perams):
    count, _, spins, nvec, columns = perams.shape
    return pl.pallas_call(
        flip_kernel,
        grid=(count, spins),
        in_specs=[pl.BlockSpec((1, 2, 1, nvec, columns), lambda k, s: (k, 0, s, 0, 0))],
        out_specs=pl.BlockSpec((1, columns, 2 * nvec), lambda k, s: (k, 0, s)),
        out_shape=jax.ShapeDtypeStruct((count, columns, spins * 2 * nvec), BF16),
        compiler_params=pltpu.CompilerParams(vmem_limit_bytes=8 << 20),
        name="transpose_tau",
    )(perams)


def pick_kernel(idx, p0, p1, p2, p3, *outs):
    for step, out in enumerate(outs):
        for k in range(2):
            for dz, piece in enumerate((p0, p1, p2, p3)):
                out[k, dz] = piece[idx[step, k]]


def pick(idx, pieces):
    rows = NVEC // YN // ZN
    vmem = lambda: pl.BlockSpec(memory_space=pltpu.VMEM)
    piece = jax.ShapeDtypeStruct((2, ZN, 2, rows, NVEC), BF16)
    return pl.pallas_call(
        pick_kernel,
        in_specs=[pl.BlockSpec(memory_space=pltpu.SMEM)] + [vmem() for _ in pieces],
        out_specs=[vmem() for _ in range(4)],
        out_shape=[piece] * 4,
        compiler_params=pltpu.CompilerParams(vmem_limit_bytes=6 << 20),
    )(idx, *pieces)


def first_row(y, z, dy, dz):
    rows = NVEC // YN // ZN
    return pl.multiple_of((y ^ dy) * (ZN * rows) + (z ^ dz) * rows, rows)


def middle_kernel(source, f0, f1, f2, f3, t_ref, tt_ref, out, fmat, gmat):
    k = pl.program_id(0)
    rows = NVEC // YN // ZN
    site = lax.axis_index("site")
    same_half = lax.axis_index("cuts") // 8 == source[0] // 2 // 8
    my_y = site // ZN
    my_z = site % ZN
    far_z = my_z ^ jnp.where(same_half, 0, 2)
    for dy, f_ref in enumerate((f0, f1, f2, f3)):
        for dz in range(ZN):
            first = first_row(my_y, far_z, dy, dz)
            f_re = f_ref[k, dz, 0]
            f_im = f_ref[k, dz, 1]
            fmat[pl.ds(first, rows), :NVEC] = f_re
            fmat[pl.ds(first, rows), NVEC:] = -f_im
            fmat[pl.ds(NVEC + first, rows), :NVEC] = f_im
            fmat[pl.ds(NVEC + first, rows), NVEC:] = f_re
    wide = t_ref.shape[-1]
    f_all = fmat[...]
    for spin in range(4):
        tau = t_ref[0, :, spin].reshape(2 * NVEC, wide)
        left = jnp.dot(f_all, tau, preferred_element_type=F32).astype(BF16)
        home = (spin + 2) % 4
        if home >= 2:
            left = -left
        base = home * 2 * NVEC
        gmat[base : base + NVEC, :wide] = left[:NVEC]
        gmat[base + NVEC : base + 2 * NVEC, :wide] = left[NVEC:]
        gmat[base : base + NVEC, wide:] = left[NVEC:]
        gmat[base + NVEC : base + 2 * NVEC, wide:] = -left[:NVEC]
    out[0] = jnp.dot(tt_ref[0], gmat[...], preferred_element_type=F32).astype(BF16)


def middle_of(source_slice, source, perams, perams_t):
    count, _, spins, nvec, wide = perams.shape
    rows = NVEC // YN // ZN
    f_spec = lambda: pl.BlockSpec((count, ZN, 2, rows, NVEC), lambda k, *_: (0, 0, 0, 0, 0))
    return pl.pallas_call(
        middle_kernel,
        grid_spec=pltpu.PrefetchScalarGridSpec(
            num_scalar_prefetch=1,
            grid=(count,),
            in_specs=[f_spec() for _ in range(4)]
            + [
                pl.BlockSpec((1, 2, spins, nvec, wide), lambda k, *_: (k, 0, 0, 0, 0)),
                pl.BlockSpec((1, wide, spins * 2 * nvec), lambda k, *_: (k, 0, 0)),
            ],
            out_specs=pl.BlockSpec((1, wide, 2 * wide), lambda k, *_: (k, 0, 0)),
            scratch_shapes=[
                pltpu.VMEM((2 * NVEC, 2 * NVEC), BF16),
                pltpu.VMEM((spins * 2 * nvec, 2 * wide), BF16),
            ],
        ),
        out_shape=jax.ShapeDtypeStruct((count, wide, 2 * wide), BF16),
        compiler_params=pltpu.CompilerParams(vmem_limit_bytes=36 << 20),
        name="middle",
    )(source_slice, *source, perams, perams_t)


def table_at(row, column):
    shared = row & column
    return jnp.where(((shared & 1) ^ (shared >> 1)) == 1, -0.5, 0.5)


def outer_kernel(order, s0, s1, s2, s3, m_ref, out, smat):
    k = pl.program_id(0)
    rows = NVEC // YN // ZN
    site = lax.axis_index("site")
    my_y = site // ZN
    my_z = site % ZN

    @pl.when(pl.program_id(1) == 0)
    def _():
        for dy, s_ref in enumerate((s0, s1, s2, s3)):
            for dz in range(ZN):
                first = first_row(my_y, my_z, dy, dz)
                s_re = s_ref[k, dz, 0]
                s_im = s_ref[k, dz, 1]
                smat[pl.ds(first, rows), :NVEC] = s_re
                smat[pl.ds(first, rows), NVEC:] = s_im
                smat[pl.ds(NVEC + first, rows), :NVEC] = -s_im
                smat[pl.ds(NVEC + first, rows), NVEC:] = s_re

    wide = m_ref.shape[2] // 2
    s_all = smat[...]
    inner = []
    for e in range(2):
        block = jnp.concatenate(
            [
                m_ref[0, :, e * NVEC : (e + 1) * NVEC],
                m_ref[0, :, wide + e * NVEC : wide + (e + 1) * NVEC],
            ],
            axis=1,
        )
        inner.append(jnp.dot(block, s_all, preferred_element_type=F32))
    for f in range(2):
        mixed = inner[0] * table_at(order[0], order[f]) + inner[1] * table_at(order[1], order[f])
        out[0, 0, :, f * NVEC : (f + 1) * NVEC] = mixed[:, :NVEC].astype(BF16)
        out[0, 1, :, f * NVEC : (f + 1) * NVEC] = mixed[:, NVEC:].astype(BF16)


def correlators_of(spin_order, sinks, middle):
    count, wide, _ = middle.shape
    rows = NVEC // YN // ZN
    s_spec = lambda: pl.BlockSpec((count, ZN, 2, rows, NVEC), lambda k, *_: (0, 0, 0, 0, 0))
    return pl.pallas_call(
        outer_kernel,
        grid_spec=pltpu.PrefetchScalarGridSpec(
            num_scalar_prefetch=1,
            grid=(count, 2),
            in_specs=[s_spec() for _ in range(4)]
            + [pl.BlockSpec((1, wide // 2, 2 * wide), lambda k, j, *_: (k, j, 0))],
            out_specs=pl.BlockSpec((1, 2, wide // 2, wide), lambda k, j, *_: (k, 0, j, 0)),
            scratch_shapes=[pltpu.VMEM((2 * NVEC, 2 * NVEC), BF16)],
        ),
        out_shape=jax.ShapeDtypeStruct((count, 2, wide, wide), BF16),
        compiler_params=pltpu.CompilerParams(vmem_limit_bytes=16 << 20),
        name="outer",
    )(spin_order, *sinks, middle)


def body(
    eigen_vectors, perambulators, momenta, source_slice, sink_slices, sink_momenta, spin_order
):
    slab_slices = eigen_vectors.shape[0]
    site_count = eigen_vectors.shape[-1]
    cut = lax.axis_index("cuts")
    source = source_slice[0]
    root = source // slab_slices
    near = source % slab_slices
    root_h = root // 8
    root_x = root // 2 % 4
    flat = (sink_slices != near).astype(jnp.int32) * NMOM + sink_momenta
    vectors = eigen_vectors.swapaxes(3, 4).reshape(slab_slices, 2, 3 * site_count, NVEC)

    def swap_y(parts):
        got = {}
        for step in (2, 1, 3):
            got[step] = lax.ppermute(parts[step], "site", y_swap(step))
        return [got[1], got[2], got[3]]

    def swap_z(parts):
        return [lax.ppermute(parts[step], "site", z_swap(step)) for step in (1, 2, 3)]

    def reduce_slice(turned):
        parts = partial_elementals(
            turned, source_slice, momenta, sink_slices, sink_momenta, vectors
        )
        got = swap_y(parts)
        notes = got
        parts = sum_and_split(parts[0], got)
        got = swap_z(parts)
        chunk = (parts[0] + sum(g.astype(F32) for g in got)).astype(BF16)
        return chunk.reshape(NMOM, 2, NVEC // YN // ZN, NVEC), notes

    chunk_a, notes = reduce_slice(False)
    chunk_b, _ = reduce_slice(True)
    tall = 2 * NMOM * NVEC // YN
    idx = jnp.stack([flat] + [v[tall : tall + 2, 0].astype(jnp.int32) for v in notes])

    held = chunk_a
    my_x = cut // 2 % 4
    for step in (1, 2, 3):
        got = lax.ppermute(chunk_a, "cuts", cut_swap(step, 0))
        held = jnp.where((my_x ^ step) == root_x, got, held)
    got = lax.ppermute(held, ("site", "cuts"), half_swap())
    held = jnp.where(cut // 8 == root_h, held, got)
    got = lax.ppermute(held, "cuts", cut_swap(0, 1))
    held = jnp.where(cut % 2 == root % 2, held, got)

    pieces = [held] + swap_z([held] * 4)
    parts = pick(idx % NMOM, pieces)
    source_parts = [parts[0]] + swap_y(parts)
    own_ab = jnp.concatenate([chunk_a, chunk_b], axis=0)
    pieces = [own_ab] + swap_z([own_ab] * 4)
    pieces, _ = lax.optimization_barrier((pieces, parts))
    parts = pick(idx, pieces)
    sink_parts = [parts[0]] + swap_y(parts)

    count = perambulators.shape[0]
    perams = perambulators.reshape(count, 2, 4, NVEC, 2 * NVEC)
    perams_t = transposed(perams)
    middle = middle_of(source_slice, source_parts, perams, perams_t)
    return correlators_of(spin_order, sink_parts, middle)


def solution(mesh):
    placed = (
        P("cuts", None, None, None, "site"),
        P(("site", "cuts"), None, None, None),
        P(),
        P(),
        P(("site", "cuts")),
        P(("site", "cuts")),
        P(),
    )
    return jax.shard_map(
        body,
        mesh=mesh,
        in_specs=placed,
        out_specs=P(("site", "cuts"), None, None, None),
        check_vma=False,
    )
```
